128 devices in a mesh: gx: 16 (over z, y_hi, core), gy: 8 (over y_lo, x).
Axes of the slice: x: 4, y: 4 (y_hi: 2, y_lo: 2; y = y_hi * 2 + y_lo), z: 4, core: 2. Of those that a mesh axis runs over, the one named last changes fastest.
Arguments:
- features: bfloat16 [16, 8, 32, 64, 256], P('gx', 'gy'), may hold values from -6 to 6
- weights: bfloat16 [27, 256, 256], replicated, may hold values from -0.078125 to 0.078125
- cotangent: bfloat16 [16, 8, 32, 64, 256], P('gx', 'gy'), may hold values from -6 to 6
- send_lists: int32 [16, 8, 8, 8], P('gx', 'gy'), may hold values from 0 to 31, as said below
- block_offset: int32 [16, 8, 108], P('gx', 'gy'), may hold values from 0 to 26, as said below
- block_input: int32 [16, 8, 108, 8], P('gx', 'gy'), may hold values from 0 to 95, as said below
- block_output: int32 [16, 8, 108, 8], P('gx', 'gy'), may hold values from 0 to 32, as said below
- block_count: int32 [16, 8], P('gx', 'gy'), may hold values from 1 to 108, as said below
Outputs:
- out_features: bfloat16 [16, 8, 32, 64, 256], P('gx', 'gy')
- feat_grad: bfloat16 [16, 8, 32, 64, 256], P('gx', 'gy')
- weight_grad: float32 [27, 256, 256], replicated
The draws below stay inside these ranges and needn't reach their ends.
Inputs may be any that keep to these rules, and one draw needn't show every extreme that they name: `send_lists`: each of a device's 8 lists names 8 different tiles that the device holds. `block_offset`: 0 in blocks past block_count. `block_input`: a tile slot of the device or a halo slot as in the reference program; 0 in unused pairs. `block_output`: 32 marks an unused pair; a device's used pairs of one offset name different tiles; the used blocks come first, grouped by offset, and blocks past block_count hold only unused pairs. `block_count`: some device uses all 108 blocks.
All inputs are finite; a program needn't handle non-finite values.
Results may differ from the reference program's by a relative error of at most 0.0029.
Values may be sent and summed in bfloat16 or wider, within the bound.
A program may use at most 128 MiB of HBM per device.

```python
import math
import jax
import jax.numpy as jnp
from jax import lax

CHANNELS = 256
VOXELS = 64
OFFSETS = 27
BLOCK = 8
TILES_DEV = 32
HALO = 8
PER_OFFSET = 4
BLOCKS = 108
SLABS_X = 16
SLABS_Y = 8
TILES_ALL = 4096


def device_plan(key, active, dense):
    keys = jax.random.split(key, 7)
    slots = jnp.arange(TILES_DEV, dtype=jnp.int32)

    def ordering(order_key):
        noise = jax.random.randint(order_key, (TILES_DEV,), 0, 4096)
        score = noise * (2 * TILES_DEV) + slots + jnp.where(slots >= active, 4096 * 2 * TILES_DEV, 0)
        return jnp.argsort(score).astype(jnp.int32)
    orders = jax.vmap(ordering)(jax.random.split(keys[0], OFFSETS))
    sends = jax.vmap(ordering)(jax.random.split(keys[1], 8))[:, :HALO]
    counts = jax.random.randint(keys[2], (OFFSETS,), -(active // 2), active + 1)
    counts = jnp.maximum(counts, 0)
    counts = jnp.where(dense, TILES_DEV, counts)
    counts = counts.at[OFFSETS // 2].set(active)
    place = jnp.arange(PER_OFFSET * BLOCK, dtype=jnp.int32).reshape(PER_OFFSET, BLOCK)
    used = place[None] < counts[:, None, None]
    picked = orders[:, jnp.minimum(place, TILES_DEV - 1).reshape(-1)].reshape(OFFSETS, PER_OFFSET, BLOCK)
    outputs = jnp.where(used, picked, TILES_DEV)
    shape = (OFFSETS, PER_OFFSET, BLOCK)
    from_halo = jax.random.randint(keys[3], shape, 0, 4) == 0
    halo_slot = jax.random.randint(keys[4], shape, TILES_DEV, TILES_DEV + 8 * HALO)
    local_slot = jax.random.randint(keys[5], shape, 0, active)
    inputs = jnp.where(from_halo, halo_slot, local_slot)
    center = (jnp.arange(OFFSETS) == OFFSETS // 2)[:, None, None]
    inputs = jnp.where(center, picked, inputs)
    inputs = inputs.at[OFFSETS // 2, 0, 0].set(TILES_DEV + 8 * HALO - 1)
    inputs = jnp.where(used, inputs, 0)
    group_score = jax.random.randint(keys[6], (OFFSETS,), 0, 4096) * OFFSETS + jnp.arange(OFFSETS)
    group_place = jnp.argsort(jnp.argsort(group_score))
    live = (place[None, :, 0] < counts[:, None]).reshape(-1)
    block_index = jnp.arange(BLOCKS)
    rank = jnp.where(live, 0, 1) * BLOCKS + group_place[block_index // PER_OFFSET] * PER_OFFSET + block_index % PER_OFFSET
    order = jnp.argsort(rank)
    offsets = jnp.where(live, jnp.repeat(jnp.arange(OFFSETS), PER_OFFSET), 0)[order]
    block_in = inputs.reshape(BLOCKS, BLOCK)[order]
    block_out = outputs.reshape(BLOCKS, BLOCK)[order]
    return (sends.astype(jnp.int32), offsets.astype(jnp.int32), block_in.astype(jnp.int32), block_out.astype(jnp.int32), jnp.sum(live).astype(jnp.int32))


def plan(key):
    keys = jax.random.split(jax.random.fold_in(key, 11), 4)
    devices_all = SLABS_X * SLABS_Y
    dense = jax.random.randint(keys[0], (devices_all,), 0, 4) == 0
    chosen = jax.random.randint(keys[1], (), 0, devices_all)
    dense = dense | (jnp.arange(devices_all) == chosen)
    light = jax.random.randint(keys[2], (devices_all,), TILES_DEV // 3, TILES_DEV // 2 + 1)
    active = jnp.where(dense, TILES_DEV, light)
    pieces = jax.vmap(device_plan)(jax.random.split(keys[3], devices_all), active, dense)
    return [piece.reshape((SLABS_X, SLABS_Y) + piece.shape[1:]) for piece in pieces]


def draw_send_lists(key, part):
    return plan(key)[0]


def draw_block_offset(key, part):
    return plan(key)[1]


def draw_block_input(key, part):
    return plan(key)[2]


def draw_block_output(key, part):
    return plan(key)[3]


def draw_block_count(key, part):
    return plan(key)[4]


def steps_of(stream_key, dims, cuts, low, largest):
    def one(position, shards_of):
        draws = jax.random.uniform(jax.random.fold_in(jax.random.fold_in(stream_key, 6), position), (shards_of,), jnp.float32, low / len(cuts), largest / len(cuts))
        return jnp.repeat(jnp.exp(draws), dims[position] // shards_of).reshape((-1,) + (1,) * (len(dims) - position - 1))

    gain = one(*cuts[0])
    for cut in cuts[1:]:
        gain = gain * one(*cut)
    return gain


def scatter_about(key, extent, width, limit, shards=(), kind=jnp.bfloat16):
    level = steps_of(key, extent, shards, -0.22, 0.18) if shards else 1.0
    values = jax.random.normal(key, extent, jnp.float32) * width * level
    return jnp.minimum(jnp.maximum(values, -limit), limit).astype(kind)


def setup_inputs(seed: int = 0) -> dict:
    streams_of = jax.random.split(jax.random.key(seed), 9)
    features = scatter_about(streams_of[0], (SLABS_X, SLABS_Y, TILES_DEV, VOXELS, CHANNELS), 1.0, 6.0, ((0, 16), (1, 8)))
    weights = scatter_about(streams_of[1], (OFFSETS, CHANNELS, CHANNELS), (OFFSETS * CHANNELS) ** -0.5, 0.078125)
    cotangent = scatter_about(streams_of[2], (SLABS_X, SLABS_Y, TILES_DEV, VOXELS, CHANNELS), 1.0, 6.0, ((0, 16), (1, 8)))
    send_lists = draw_send_lists(jax.random.fold_in(streams_of[8], 71), 0)
    block_offset = draw_block_offset(jax.random.fold_in(streams_of[8], 71), 0)
    block_input = draw_block_input(jax.random.fold_in(streams_of[8], 71), 0)
    block_output = draw_block_output(jax.random.fold_in(streams_of[8], 71), 0)
    block_count = draw_block_count(jax.random.fold_in(streams_of[8], 71), 0)
    return {"features": features, "weights": weights, "cotangent": cotangent, "send_lists": send_lists, "block_offset": block_offset, "block_input": block_input, "block_output": block_output, "block_count": block_count}


DIRECTIONS = ((-1, -1), (-1, 0), (-1, 1), (0, -1), (0, 1), (1, -1), (1, 0), (1, 1))

def neighbour(array, step_x, step_y):
    rolled = jnp.roll(array, (step_x, step_y), axis=(0, 1))
    first = jnp.arange(array.shape[0]) - step_x
    second = jnp.arange(array.shape[1]) - step_y
    inside = ((first >= 0) & (first < array.shape[0]))[:, None] & ((second >= 0) & (second < array.shape[1]))[None, :]
    inside = inside.reshape(inside.shape + (1,) * (array.ndim - 2))
    return jnp.where(inside, rolled, jnp.zeros_like(rolled))

def by_device(array):
    return array.reshape((SLABS_X * SLABS_Y,) + array.shape[2:])

def take_rows(table, places):
    return table[places]

def add_rows(target, places, values):
    return target.at[places].add(values)

def reference(features, weights, cotangent, send_lists, block_offset, block_input, block_output, block_count):
    packets = jax.vmap(jax.vmap(take_rows))(features, send_lists)
    halos = jnp.stack([neighbour(packets[:, :, which], pair[0], pair[1]) for which, pair in enumerate(DIRECTIONS)], axis=2)
    extended = jnp.concatenate([features, halos.reshape(SLABS_X, SLABS_Y, 8 * HALO, VOXELS, CHANNELS)], axis=2)
    live = jnp.arange(BLOCKS)[None, None, :, None] < block_count[:, :, None, None]
    outputs = jnp.where(live, block_output, TILES_DEV).astype(jnp.int32)

    def forward_device(item):
        ext, offsets, inputs, targets = item

        def step(accum, blocks):
            offset, source, target = blocks
            gathered = ext[source].reshape(BLOCK * VOXELS, CHANNELS)
            product = jnp.dot(gathered, weights[offset], preferred_element_type=jnp.float32)
            return (accum.at[target].add(product.reshape(BLOCK, VOXELS, CHANNELS), mode='drop'), None)
        result, _ = lax.scan(step, jnp.zeros((TILES_DEV, VOXELS, CHANNELS), jnp.float32), (offsets, inputs, targets))
        return result
    items = (by_device(extended), by_device(block_offset), by_device(block_input), by_device(outputs))
    pre = lax.map(forward_device, items).reshape(features.shape)
    sigma = jax.nn.sigmoid(pre)
    out_features = (features.astype(jnp.float32) + pre * sigma).astype(jnp.bfloat16)
    pre_grad = (cotangent.astype(jnp.float32) * sigma * (1.0 + pre * (1.0 - sigma))).astype(jnp.bfloat16)
    padded_grad = jnp.concatenate([pre_grad, jnp.zeros((SLABS_X, SLABS_Y, 1, VOXELS, CHANNELS), jnp.bfloat16)], axis=2)

    def backward_device(weight_sum, item):
        ext, grads, offsets, inputs, targets = item

        def step(carry, blocks):
            ext_grad, partial_value = carry
            offset, source, target = blocks
            gathered = ext[source].reshape(BLOCK * VOXELS, CHANNELS)
            incoming = grads[target].reshape(BLOCK * VOXELS, CHANNELS)
            back = jnp.dot(incoming, weights[offset].T, preferred_element_type=jnp.float32)
            ext_grad = ext_grad.at[source].add(back.reshape(BLOCK, VOXELS, CHANNELS))
            partial_value = partial_value.at[offset].add(jnp.dot(gathered.T, incoming, preferred_element_type=jnp.float32))
            return ((ext_grad, partial_value), None)
        start = jnp.zeros((TILES_DEV + 8 * HALO, VOXELS, CHANNELS), jnp.float32)
        (ext_grad, weight_sum), _ = lax.scan(step, (start, weight_sum), (offsets, inputs, targets))
        return (weight_sum, ext_grad)
    items = (by_device(extended), by_device(padded_grad), by_device(block_offset), by_device(block_input), by_device(outputs))
    weight_sum, ext_grad = lax.scan(backward_device, jnp.zeros((OFFSETS, CHANNELS, CHANNELS), jnp.float32), items)
    ext_grad = ext_grad.reshape(SLABS_X, SLABS_Y, TILES_DEV + 8 * HALO, VOXELS, CHANNELS)
    adjoints = ext_grad[:, :, TILES_DEV:].reshape(SLABS_X, SLABS_Y, 8, HALO, VOXELS, CHANNELS)
    feat_sum = cotangent.astype(jnp.float32) + ext_grad[:, :, :TILES_DEV]
    for which, pair in enumerate(DIRECTIONS):
        returned = neighbour(adjoints[:, :, which], -pair[0], -pair[1])
        feat_sum = jax.vmap(jax.vmap(add_rows))(feat_sum, send_lists[:, :, which], returned)
    feat_grad = feat_sum.astype(jnp.bfloat16)
    weight_grad = weight_sum / math.sqrt(VOXELS * TILES_ALL)
    return (out_features, feat_grad, weight_grad)
```

```python
import functools
import math

import jax
import jax.numpy as jnp
from jax import lax
from jax.experimental import pallas as pl
from jax.experimental.pallas import tpu as pltpu
from jax.sharding import PartitionSpec as P

MESH = pl.DeviceIdType.MESH
DIRECTIONS = ((-1, -1), (-1, 0), (-1, 1), (0, -1), (0, 1), (1, -1), (1, 0), (1, 1))
K, T, V, C, H = 27, 32, 64, 256, 64
S = T + H
GX, GY = 16, 8
BF, F32 = jnp.bfloat16, jnp.float32
ORDERS = (("z", "x", "y"), ("x", "y", "z"), ("y", "z", "x"))
GROUPS, PER = 3, 9


def vmem():
    return pl.BlockSpec(memory_space=pltpu.VMEM)


def smem():
    return pl.BlockSpec(memory_space=pltpu.SMEM)


class Place:
    def __init__(self):
        self.i, self.j = lax.axis_index("gx"), lax.axis_index("gy")
        core = self.i % 2
        self.at = {"core": core, "x": self.j % 4, "z": self.i // 4, "y": ((self.i // 2) % 2) * 2 + self.j // 4}

    def device(self, **moved):
        c = {**self.at, **moved}
        return {"gx": c["z"] * 4 + (c["y"] // 2) * 2 + c["core"], "gy": (c["y"] % 2) * 4 + c["x"]}

    def inside(self, a, b):
        p, q = self.i + a, self.j + b
        return (p >= 0) & (p < GX) & (q >= 0) & (q < GY)

    def neighbour(self, a, b):
        return {"gx": jnp.clip(self.i + a, 0, GX - 1), "gy": jnp.clip(self.j + b, 0, GY - 1)}


def greet_neighbours(place, bar):
    count = 0
    for a, b in DIRECTIONS:
        @pl.when(place.inside(a, b))
        def _():
            pl.semaphore_signal(bar, inc=1, device_id=place.neighbour(a, b), device_id_type=MESH)

        count = count + jnp.where(place.inside(a, b), 1, 0)
    return count


def exchange_start(place, d, sign, src, dst, ssem, rsem):
    a, b = sign * DIRECTIONS[d][0], sign * DIRECTIONS[d][1]
    copy = pltpu.make_async_remote_copy(
        src_ref=src.at[d], dst_ref=dst.at[d], send_sem=ssem.at[d], recv_sem=rsem.at[d],
        device_id=place.neighbour(a, b), device_id_type=MESH)
    return copy, place.inside(a, b), place.inside(-a, -b)


def halo_kernel(lists, x, halo, pack, ssem, rsem):
    place = Place()
    bar = pltpu.get_barrier_semaphore()
    pl.semaphore_wait(bar, greet_neighbours(place, bar))
    order = (0, 2, 5, 7, 1, 6, 3, 4)
    for d in order:
        for h in range(8):
            pack[d, h] = x[lists[d, h]]
        copy, to, _ = exchange_start(place, d, 1, pack, halo, ssem, rsem)

        @pl.when(to)
        def _():
            copy.start()

    for d in order:
        copy, to, come = exchange_start(place, d, 1, pack, halo, ssem, rsem)

        @pl.when(come)
        def _():
            copy.wait_recv()

        @pl.when(jnp.logical_not(come))
        def _():
            halo[d] = jnp.zeros(halo.shape[1:], halo.dtype)

        @pl.when(to)
        def _():
            copy.wait_send()


def halo_exchange(lists, x):
    return pl.pallas_call(
        halo_kernel, out_shape=jax.ShapeDtypeStruct((8, 8, V, C), BF),
        in_specs=[smem(), vmem()], out_specs=vmem(),
        scratch_shapes=[pltpu.VMEM((8, 8, V, C), BF), pltpu.SemaphoreType.DMA((8,)), pltpu.SemaphoreType.DMA((8,))],
        name="halo",
        compiler_params=pltpu.CompilerParams(collective_id=0, has_side_effects=True, vmem_limit_bytes=32 << 20),
    )(lists, x)


def local_kernel(tab, x, halo, w, cot, outf, adj, loc, ext, pg, pre, acc):
    ext[:T] = x[...]
    ext[T:S] = halo[...]
    ext[S] = jnp.zeros((V, C), BF)
    pre[...] = jnp.zeros_like(pre)

    def forward(k, _):
        wk = w[k]
        for g in range(0, T, 8):
            rows = jnp.concatenate([ext[tab[k, g + n]] for n in range(8)], axis=0)
            pre[pl.ds(g * V, 8 * V), :] += jnp.dot(rows, wk, preferred_element_type=F32)
        return 0

    lax.fori_loop(0, K, forward, 0)

    def activate(t, _):
        p = pre[pl.ds(t * V, V), :]
        s = jax.nn.sigmoid(p)
        outf[t] = (x[t].astype(F32) + p * s).astype(BF)
        pg[pl.ds(t * V, V), :] = (cot[t].astype(F32) * s * (1.0 + p * (1.0 - s))).astype(BF)
        return 0

    lax.fori_loop(0, T, activate, 0)
    acc[...] = jnp.zeros_like(acc)

    def backward(k, _):
        wk = w[k]
        for g in range(0, T, 8):
            z = lax.dot_general(pg[pl.ds(g * V, 8 * V), :], wk, (((1,), (1,)), ((), ())), preferred_element_type=F32)
            for n in range(8):
                s = tab[k, g + n]
                acc[s] = acc[s] + z[n * V:(n + 1) * V]
        return 0

    lax.fori_loop(0, K, backward, 0)
    loc[...] = acc[:T] + cot[...].astype(F32)
    adj[...] = acc[T:S].astype(BF)


def local_part(tab, x, halo, w, cot):
    return pl.pallas_call(
        local_kernel,
        out_shape=(jax.ShapeDtypeStruct((T, V, C), BF), jax.ShapeDtypeStruct((H, V, C), BF),
                   jax.ShapeDtypeStruct((T, V, C), F32), jax.ShapeDtypeStruct((S + 1, V, C), BF),
                   jax.ShapeDtypeStruct((T * V, C), BF)),
        in_specs=[smem()] + [vmem()] * 4, out_specs=(vmem(),) * 5,
        scratch_shapes=[pltpu.VMEM((T * V, C), F32), pltpu.VMEM((S + 1, V, C), F32)],
        name="local",
        compiler_params=pltpu.CompilerParams(vmem_limit_bytes=56 << 20),
    )(tab, x, halo, w, cot)


def grad_kernel(tab, ext, pg, adj, ret, ag, wbuf, prec, sa, ra, sums_a, rb, sums_b, rc,
                hs, hr, ps, pr, as_, ar, bs, br, cs, cr, gcs, gcr, gbs, gbr, gas, gar, ges, ger):
    place = Place()
    core = place.at["core"]
    partner = place.device(core=1 - core)
    bar = pltpu.get_barrier_semaphore()
    count = greet_neighbours(place, bar)
    pl.semaphore_signal(bar, inc=1, device_id=partner, device_id_type=MESH)
    for axis in ("x", "y", "z"):
        for p in (1, 2, 3):
            pl.semaphore_signal(bar, inc=1, device_id=place.device(**{axis: (place.at[axis] + p) % 4}), device_id_type=MESH)
    pl.semaphore_wait(bar, count + 10)

    order = (0, 2, 5, 7, 1, 6, 3, 4)
    for d in order:
        copy, to, _ = exchange_start(place, d, -1, adj, ret, hs, hr)

        @pl.when(to)
        def _():
            copy.start()

    def remote(src, dst, send, recv, to):
        return pltpu.make_async_remote_copy(src_ref=src, dst_ref=dst, send_sem=send, recv_sem=recv, device_id=to, device_id_type=MESH)

    def to_partner(k):
        return remote(wbuf.at[k, pl.ds((1 - core) * 128, 128)], prec.at[k], ps.at[k], pr.at[k], partner)

    def where(g, n):
        axis = ORDERS[g][n]
        mine = place.at[axis]
        return mine, lambda p: (mine + p) % 4, lambda p: place.device(**{axis: (mine + p) % 4})

    def compute(g):
        def step(k, _):
            rows = jnp.concatenate([ext[tab[k, t]] for t in range(T)], axis=0)
            wbuf[k] = lax.dot_general(rows, pg[...], (((0,), (0,)), ((), ())), preferred_element_type=F32)
            to_partner(k).start()
            return 0

        lax.fori_loop(PER * g, PER * (g + 1), step, 0)

    def a_copy(g, p):
        return remote(sa.at[g, p - 1], ra.at[g, p - 1], as_.at[g, p - 1], ar.at[g, p - 1], where(g, 0)[2](p))

    def pack_a(g):
        mine, other, _ = where(g, 0)

        def step(n, _):
            k = PER * g + n
            to_partner(k).wait_recv()
            for p in (1, 2, 3):
                r = other(p) * 32
                sa[g, p - 1, n] = (wbuf[k, pl.ds(core * 128 + r, 32)] + prec[k, pl.ds(r, 32)]).astype(BF)
            return 0

        lax.fori_loop(0, PER, step, 0)
        for p in (1, 2, 3):
            a_copy(g, p).start()

    def b_copy(g, p):
        _, other, to = where(g, 1)
        return remote(sums_a.at[g, :, pl.ds(other(p) * 8, 8)], rb.at[g, p - 1], bs.at[g, p - 1], br.at[g, p - 1], to(p))

    def finish_a(g):
        mine = where(g, 0)[0]
        for p in (1, 2, 3):
            a_copy(g, p).wait_recv()

        def step(n, _):
            k = PER * g + n
            r = mine * 32
            total = wbuf[k, pl.ds(core * 128 + r, 32)] + prec[k, pl.ds(r, 32)]
            for p in (1, 2, 3):
                total = total + ra[g, p - 1, n].astype(F32)
            sums_a[g, n] = total
            return 0

        lax.fori_loop(0, PER, step, 0)
        for p in (1, 2, 3):
            b_copy(g, p).start()

    def c_copy(g, p):
        _, other, to = where(g, 2)
        first = jnp.minimum(other(p), 2) * 3
        return remote(sums_b.at[g, pl.ds(first, 3)], rc.at[g, p - 1], cs.at[g, p - 1], cr.at[g, p - 1], to(p)), other(p) < 3

    def finish_b(g):
        mine = where(g, 1)[0]
        for p in (1, 2, 3):
            b_copy(g, p).wait_recv()
        total = sums_a[g, :, pl.ds(mine * 8, 8)]
        for p in (1, 2, 3):
            total = total + rb[g, p - 1]
        sums_b[g] = total
        for p in (1, 2, 3):
            copy, to = c_copy(g, p)

            @pl.when(to)
            def _():
                copy.start()

    def gc_copy(g, p, owner):
        a, b, c = (where(g, n)[0] for n in range(3))
        block = ag.at[g, core, a, b, jnp.minimum(owner, 2)]
        return remote(block, block, gcs.at[g, p - 1], gcr.at[g, p - 1], where(g, 2)[2](p))

    def finish_c(g):
        a, b, c = (where(g, n)[0] for n in range(3))

        @pl.when(c < 3)
        def _():
            for p in (1, 2, 3):
                c_copy(g, p)[0].wait_recv()
            total = sums_b[g, pl.ds(jnp.minimum(c, 2) * 3, 3)]
            for p in (1, 2, 3):
                total = total + rc[g, p - 1]
            ag[g, core, a, b, jnp.minimum(c, 2)] = total.reshape(24, C).astype(BF)
            for p in (1, 2, 3):
                gc_copy(g, p, c).start()

    def gb_copy(g, p, owner):
        a = where(g, 0)[0]
        block = ag.at[g, core, a, owner]
        return remote(block, block, gbs.at[g, p - 1], gbr.at[g, p - 1], where(g, 1)[2](p))

    def gather_b(g):
        mine, other, _ = where(g, 2)
        for p in (1, 2, 3):
            owner = other(4 - p)

            @pl.when(owner < 3)
            def _():
                gc_copy(g, p, owner).wait_recv()

        for p in (1, 2, 3):
            gb_copy(g, p, where(g, 1)[0]).start()

    def ga_copy(g, p, owner):
        block = ag.at[g, core, owner]
        return remote(block, block, gas.at[g, p - 1], gar.at[g, p - 1], where(g, 0)[2](p))

    def ge_copy(g, p, half, owner):
        block = ag.at[g, half, owner]
        return remote(block, block, ges.at[g, p], ger.at[g, p], partner)

    def gather_a(g):
        other = where(g, 1)[1]
        for p in (1, 2, 3):
            gb_copy(g, p, other(4 - p)).wait_recv()
        mine = where(g, 0)[0]
        for p in (1, 2, 3):
            ga_copy(g, p, mine).start()
        ge_copy(g, 0, core, mine).start()

    def gather_core(g):
        other = where(g, 0)[1]
        for p in (1, 2, 3):
            ga_copy(g, p, other(4 - p)).wait_recv()
            ge_copy(g, p, core, other(4 - p)).start()

    compute(0)
    pack_a(0)
    compute(1)
    finish_a(0)
    pack_a(1)
    compute(2)
    finish_b(0)
    finish_a(1)
    pack_a(2)
    finish_c(0)
    finish_b(1)
    finish_a(2)
    gather_b(0)
    finish_c(1)
    finish_b(2)
    gather_a(0)
    gather_b(1)
    finish_c(2)
    gather_core(0)
    gather_a(1)
    gather_b(2)
    gather_core(1)
    gather_a(2)
    gather_core(2)

    for d in order:
        copy, to, come = exchange_start(place, d, -1, adj, ret, hs, hr)

        @pl.when(come)
        def _():
            copy.wait_recv()

        @pl.when(jnp.logical_not(come))
        def _():
            ret[d] = jnp.zeros(ret.shape[1:], ret.dtype)

        @pl.when(to)
        def _():
            copy.wait_send()

    def drain(k, _):
        to_partner(k).wait_send()
        return 0

    lax.fori_loop(0, K, drain, 0)
    for g in range(GROUPS):
        mine = [where(g, n)[0] for n in range(3)]
        for p in (1, 2, 3):
            a_copy(g, p).wait_send()
            b_copy(g, p).wait_send()
            copy, to = c_copy(g, p)

            @pl.when(to)
            def _():
                copy.wait_send()

            @pl.when(mine[2] < 3)
            def _():
                gc_copy(g, p, mine[2]).wait_send()

            gb_copy(g, p, mine[1]).wait_send()
            ga_copy(g, p, mine[0]).wait_send()
        other = where(g, 0)[1]
        for p in range(4):
            ge_copy(g, p, core, other(4 - p)).wait_send()
            ge_copy(g, p, 1 - core, other(4 - p)).wait_recv()


def grad_part(tab, ext, pg, adj):
    dma = pltpu.SemaphoreType.DMA
    return pl.pallas_call(
        grad_kernel,
        out_shape=(jax.ShapeDtypeStruct((8, 8, V, C), BF), jax.ShapeDtypeStruct((GROUPS, 2, 4, 4, 3, 24, C), BF)),
        in_specs=[smem()] + [vmem()] * 3, out_specs=(vmem(), vmem()),
        scratch_shapes=[
            pltpu.VMEM((K, C, C), F32), pltpu.VMEM((K, 128, C), F32),
            pltpu.VMEM((GROUPS, 3, PER, 32, C), BF), pltpu.VMEM((GROUPS, 3, PER, 32, C), BF),
            pltpu.VMEM((GROUPS, PER, 32, C), F32), pltpu.VMEM((GROUPS, 3, PER, 8, C), F32),
            pltpu.VMEM((GROUPS, PER, 8, C), F32), pltpu.VMEM((GROUPS, 3, 3, 8, C), F32),
            dma((8,)), dma((8,)), dma((K,)), dma((K,))]
            + [dma((GROUPS, 3))] * 12 + [dma((GROUPS, 4))] * 2,
        name="grads",
        compiler_params=pltpu.CompilerParams(collective_id=1, has_side_effects=True, vmem_limit_bytes=56 << 20),
    )(tab, ext, pg, adj)


def feat_kernel(lists, loc, ret, out, acc):
    acc[...] = loc[...]
    for d in range(8):
        def step(h, _):
            t = lists[d, h]
            acc[t] = acc[t] + ret[d, h].astype(F32)
            return 0

        lax.fori_loop(0, 8, step, 0)
    out[...] = acc[...].astype(BF)


def feat_part(lists, loc, ret):
    return pl.pallas_call(
        feat_kernel, out_shape=jax.ShapeDtypeStruct((T, V, C), BF),
        in_specs=[smem(), vmem(), vmem()], out_specs=vmem(),
        scratch_shapes=[pltpu.VMEM((T, V, C), F32)], name="feat",
        compiler_params=pltpu.CompilerParams(vmem_limit_bytes=32 << 20),
    )(lists, loc, ret)


def widen_kernel(scale, ag, out):
    for half in range(2):
        for a in range(4):
            for b in range(4):
                for n in range(3):
                    out[n, pl.ds(half * 128 + a * 32 + b * 8, 8)] = ag[0, half, a, b, 0, pl.ds(n * 8, 8)].astype(F32) * scale


def widen_part(ag, scale):
    return pl.pallas_call(
        functools.partial(widen_kernel, scale), out_shape=jax.ShapeDtypeStruct((K, C, C), F32),
        grid=(9,),
        in_specs=[pl.BlockSpec((1, 2, 4, 4, 1, 24, C), lambda n: (n // 3, 0, 0, 0, n % 3, 0, 0))],
        out_specs=pl.BlockSpec((3, C, C), lambda n: (n, 0, 0)), name="widen",
    )(ag)


def dense_plan(block_offset, block_input, block_output, block_count):
    blocks = block_offset.shape[0]
    live = jnp.arange(blocks) < block_count
    tiles = jnp.arange(T)
    hit = (block_output[:, :, None] == tiles) & live[:, None, None]
    spread = jnp.sum(jnp.where(hit, block_input[:, :, None] - S, 0), axis=1)
    mine = jnp.arange(K)[:, None] == block_offset[None, :]
    return S + jnp.sum(jnp.where(mine[:, :, None], spread[None], 0), axis=1)


def shards(features, weights, cotangent, send_lists, block_offset, block_input, block_output, block_count):
    x, cot, lists = features[0, 0], cotangent[0, 0], send_lists[0, 0]
    halo = halo_exchange(lists, x)
    tab = dense_plan(block_offset[0, 0], block_input[0, 0], block_output[0, 0], block_count[0, 0]).astype(jnp.int32)
    outf, adj, loc, ext, pg = local_part(tab, x, halo.reshape(H, V, C), weights, cot)
    ret, ag = grad_part(tab, ext, pg, adj.reshape(8, 8, V, C))
    feat = feat_part(lists, loc, ret)
    wgrad = widen_part(ag, 1.0 / math.sqrt(V * T * GX * GY))
    return outf[None, None], feat[None, None], wgrad


def solution(mesh):
    grid = P("gx", "gy")
    return jax.shard_map(shards, mesh=mesh, in_specs=(grid, P(), grid, grid, grid, grid, grid, grid),
                         out_specs=(grid, grid, P()), check_vma=False)
```
